256 devices in a mesh: proc: 32 (over x, z), rep: 8 (over y, core).
Axes of the slice: x: 4, y: 4, z: 8, core: 2. Of those that a mesh axis runs over, the one named last changes fastest.
Arguments:
- amplitudes: bfloat16 [512, 208, 128], P('proc'), may hold values from -6 to 6
- ladder_rows: int32 [512, 8, 14], P('proc', 'rep'), may hold values from -1 to 511, as said below
- ladder_ints: bfloat16 [512, 8, 14, 128, 128], P('proc', 'rep'), may hold values from -0.046875 to 0.046875
- cycle_rows: int32 [512, 8, 8], P('proc', 'rep'), may hold values from 0 to 511, as said below
- cycle_ints: bfloat16 [512, 8, 8, 128, 128], P('proc', 'rep'), may hold values from -0.0625 to 0.0625
- bare_ints: bfloat16 [512, 208, 128], P('proc', 'rep'), may hold values from -6 to 6
- occ_energy: float32 [8, 208], replicated, may hold values from -2 to -0.5
- vir_energy: float32 [512, 128], P('proc'), may hold values from 0.5 to 4
- block_tiles: int32 [8], replicated, may hold values from 8 to 112, as said below
Outputs:
- new_amplitudes: bfloat16 [512, 208, 128], P('proc', 'rep')
The draws below stay inside these ranges and needn't reach their ends.
Inputs may be any that keep to these rules, and one draw needn't show every extreme that they name: `block_tiles`: each entry is a multiple of 8; the entries sum to 512; the irreps' tiles lie one after another in irrep order; one irrep has 112 tiles. `ladder_rows`: for a column tile l of irrep g and an index r of the second dimension, the entries list, in some order, every tile k of irrep g with k % 8 == r once; the other entries are -1. The columns of the largest irrep fill all 14 entries. `cycle_rows`: every entry at index r of the second dimension is a tile k with k % 8 == r; entries may repeat.
All inputs are finite; a program needn't handle non-finite values.
Results may differ from the reference program's by a relative error of at most 0.001.
Values may be sent and summed in bfloat16 or wider, within the bound.
No kernel may reach another device: no remote copies, remote signals or barrier semaphores. Data moves between devices by JAX's collectives and lax.ppermute only.
A program may use at most 128 MiB of HBM per device.

```python
import jax
import jax.numpy as jnp
from jax import lax

NIRREP = 8
TILE = 128
ROWS = 208
RSLOT = 8
REPLICAS = 8
KTOT = 512
UNITS = 64
MMAX = 14
LSLOT = 14
N_REP = 8


def unit_counts(key):
    folded = jax.random.fold_in(key, 11)
    subkeys = jax.random.split(folded, 2)
    leftover = UNITS - MMAX - (NIRREP - 1)
    extras = jnp.zeros((NIRREP - 1,), jnp.int32)
    chosen = jax.random.randint(subkeys[0], (max(leftover, 1),), 0, NIRREP - 1)
    for position in range(leftover):
        circle = (chosen[position] + jnp.arange(NIRREP - 1, dtype=jnp.int32)) % (NIRREP - 1)
        filled = (extras[circle] >= MMAX - 1).astype(jnp.int32)
        target = circle[jnp.argmin(filled)]
        extras = extras.at[target].add(1)
    counts = jnp.concatenate([jnp.full((1,), MMAX, jnp.int32), 1 + extras])
    shuffle = jax.random.permutation(subkeys[1], NIRREP)
    return jnp.zeros((NIRREP,), jnp.int32).at[shuffle].set(counts)


def draw_block_tiles(key, part):
    return (REPLICAS * unit_counts(key)).astype(jnp.int32)


def draw_ladder_rows(key, part):
    tiles = REPLICAS * unit_counts(key)
    bounds = jnp.cumsum(tiles).astype(jnp.int32)
    starts = bounds - tiles
    columns = jnp.arange(KTOT, dtype=jnp.int32)
    irreps = jnp.sum((columns[:, None] >= bounds[None, :]).astype(jnp.int32), axis=1)
    begins = starts[irreps]
    usable = tiles[irreps] // REPLICAS
    subkeys = jax.random.split(jax.random.fold_in(key, 29), KTOT * REPLICAS)
    orders = jax.vmap(lambda single: jax.random.permutation(single, LSLOT))(subkeys).reshape(KTOT, REPLICAS, LSLOT)
    replica = jnp.arange(REPLICAS, dtype=jnp.int32)
    rows_all = begins[:, None, None] + replica[None, :, None] + REPLICAS * orders
    return jnp.where(orders < usable[:, None, None], rows_all, -1).astype(jnp.int32)


def draw_cycle_rows(key, part):
    picks = jax.random.randint(jax.random.fold_in(key, 43), (KTOT, REPLICAS, RSLOT), 0, KTOT // REPLICAS)
    replica = jnp.arange(REPLICAS, dtype=jnp.int32)
    return (replica[None, :, None] + REPLICAS * picks).astype(jnp.int32)


def steps_of(stream_key, dims, shards, least, top_value):
    def one(dim, parts):
        draws = jax.random.uniform(jax.random.fold_in(jax.random.fold_in(stream_key, 6), dim), (parts,), jnp.float32, least / len(shards), top_value / len(shards))
        return jnp.repeat(jnp.exp(draws), dims[dim] // parts).reshape((-1,) + (1,) * (len(dims) - dim - 1))

    factor_of = one(*shards[0])
    for cut in shards[1:]:
        factor_of = factor_of * one(*cut)
    return factor_of


def noise(rng, shape, deviation, reach, cuts=(), held_as=jnp.bfloat16):
    level = steps_of(rng, shape, cuts, -0.22, 0.18) if cuts else 1.0
    entries = jax.random.normal(rng, shape, jnp.float32) * deviation * level
    return jnp.minimum(jnp.maximum(entries, -reach), reach).astype(held_as)


def setup_inputs(seed: int = 0) -> dict:
    key_list = jax.random.split(jax.random.key(seed), 10)
    return {
        "amplitudes": noise(key_list[0], (KTOT, ROWS, TILE), 1.0, 6.0, ((0, 32),)),
        "ladder_rows": draw_ladder_rows(jax.random.fold_in(key_list[9], 71), 0),
        "ladder_ints": noise(key_list[2], (KTOT, REPLICAS, LSLOT, TILE, TILE), (REPLICAS * LSLOT * TILE) ** -0.5, 0.046875, ((0, 32), (1, 8))),
        "cycle_rows": draw_cycle_rows(jax.random.fold_in(key_list[9], 71), 0),
        "cycle_ints": noise(key_list[4], (KTOT, REPLICAS, RSLOT, TILE, TILE), (N_REP * RSLOT * TILE) ** -0.5, 0.0625, ((0, 32), (1, 8))),
        "bare_ints": noise(key_list[5], (KTOT, ROWS, TILE), 1.0, 6.0, ((0, 32), (1, 8))),
        "occ_energy": jnp.clip(jax.random.uniform(key_list[6], (NIRREP, ROWS), jnp.float32, -2.0, -0.5), -2.0, -0.5),
        "vir_energy": jnp.clip(0.5 + 3.5 * jax.random.uniform(key_list[7], (KTOT, TILE), jnp.float32) ** steps_of(key_list[7], (KTOT, TILE), ((0, 32),), -0.2, 0.2), 0.5, 4.0),
        "block_tiles": draw_block_tiles(jax.random.fold_in(key_list[9], 71), 0),
    }


def reference(amplitudes, ladder_rows, ladder_ints, cycle_rows, cycle_ints, bare_ints, occ_energy, vir_energy, block_tiles):
    bounds = jnp.cumsum(block_tiles).astype(jnp.int32)
    columns = jnp.arange(KTOT, dtype=jnp.int32)
    irreps = jnp.sum((columns[:, None] >= bounds[None, :]).astype(jnp.int32), axis=1).astype(jnp.int32)

    def one_column(pieces):
        lad_list, lad_tiles, cycle_list, cycle_tiles = pieces
        lad_list = lad_list.reshape(-1).astype(jnp.int32)
        usable = (lad_list >= 0).astype(jnp.float32)
        picked = amplitudes[jnp.maximum(lad_list, 0)].astype(jnp.float32) * usable[:, None, None]
        ladder = jnp.einsum("srk,skc->rc", picked, lad_tiles.reshape(-1, TILE, TILE).astype(jnp.float32))
        cycle_pick = amplitudes[cycle_list.reshape(-1).astype(jnp.int32)].astype(jnp.float32)
        cycle = jnp.einsum("srk,skc->rc", cycle_pick, cycle_tiles.reshape(-1, TILE, TILE).astype(jnp.float32))
        return ladder + cycle

    terms = lax.map(one_column, (ladder_rows, ladder_ints, cycle_rows, cycle_ints))
    residual = bare_ints.astype(jnp.float32) + terms
    denominator = vir_energy[:, None, :] - occ_energy[irreps][:, :, None]
    return (residual / denominator).astype(jnp.bfloat16)
```

```python
import jax
import jax.numpy as jnp
from jax import lax
from jax.experimental import pallas as pl
from jax.experimental.pallas import tpu as pltpu
from jax.sharding import PartitionSpec as P


NX, NZ, NY, NC = 4, 8, 4, 2
ROWS, TILE, SHARE = 208, 128, 26
LADDER, CYCLE = 14, 8
SLOTS = LADDER + CYCLE
COLS = 16
GROUP = 4
PACKED = COLS * SHARE
F32, BF16 = jnp.float32, jnp.bfloat16


def along_z(value, shift):
    pairs = [(x * NZ + z, x * NZ + (z + shift) % NZ) for x in range(NX) for z in range(NZ)]
    return lax.ppermute(value, "proc", pairs)


def along_x(value, shift):
    pairs = [(x * NZ + z, ((x + shift) % NX) * NZ + z) for x in range(NX) for z in range(NZ)]
    return lax.ppermute(value, "proc", pairs)


def along_y(value, shift):
    pairs = [(y * NC + c, ((y + shift) % NY) * NC + c) for y in range(NY) for c in range(NC)]
    return lax.ppermute(value, "rep", pairs)


def other_core(value):
    return lax.ppermute(value, "rep", [(i, i ^ 1) for i in range(NY * NC)])


def pick_kernel(where, tile, out):
    rep = where[0]
    y, c = rep // NC, rep % NC
    row = lax.broadcasted_iota(jnp.int32, (ROWS, ROWS), 0)
    col = lax.broadcasted_iota(jnp.int32, (ROWS, ROWS), 1)
    source = row
    for q in range(NY * NC):
        target_core = c if q < NY else 1 - c
        target = ((y + q) % NY) * NC + target_core
        inside = (row >= q * SHARE) & (row < (q + 1) * SHARE)
        source = jnp.where(inside, row + (target - q) * SHARE, source)
    select = (source == col).astype(F32).astype(BF16)
    out[0] = jnp.dot(select, tile[0], preferred_element_type=F32).astype(BF16)


def pick(amplitudes, rep):
    return pl.pallas_call(
        pick_kernel,
        out_shape=jax.ShapeDtypeStruct((2, ROWS, TILE), BF16),
        grid_spec=pltpu.PrefetchScalarGridSpec(
            num_scalar_prefetch=1,
            grid=(2,),
            in_specs=[pl.BlockSpec((1, ROWS, TILE), lambda j, w: (w[0] + 8 * j, 0, 0))],
            out_specs=pl.BlockSpec((1, ROWS, TILE), lambda j, w: (j, 0, 0)),
        ),
        name="pick_rows",
    )(rep, amplitudes)


def ladder_kernel(index, *refs):
    blocks = refs[:8]
    lad, cyc, keep, send, tiles, total, sems = refs[8:]
    step = pl.program_id(0)

    @pl.when(step == 0)
    def _():
        copies = []
        for n, block in enumerate(blocks):
            start = (n // 2) * 16 + (n % 2) * 10
            size = 10 if n % 2 == 0 else 6
            copies.append(
                pltpu.make_async_copy(block, tiles.at[pl.ds(start, size)], sems.at[n])
            )
        for copy in copies:
            copy.start()
        tiles[64] = jnp.zeros((ROWS, TILE), BF16)
        for copy in copies:
            copy.wait()

    for j in range(GROUP):
        base = (step * GROUP + j) * SLOTS
        acc = None
        for t in range(0, SLOTS, 2):
            left = jnp.concatenate(
                [tiles[index[base + t]], tiles[index[base + t + 1]]], axis=1
            )
            if t < LADDER:
                right = lad[j, 0, t : t + 2]
            else:
                right = cyc[j, 0, t - LADDER : t - LADDER + 2]
            term = jnp.dot(left, right.reshape(2 * TILE, TILE), preferred_element_type=F32)
            acc = term if acc is None else acc + term
        total[...] = acc
        for q in range(NY):
            keep[q, pl.ds(j * SHARE, SHARE), :] = total[pl.ds(q * SHARE, SHARE), :]
            send[q, pl.ds(j * SHARE, SHARE), :] = total[pl.ds((NY + q) * SHARE, SHARE), :]


def ladder(index, blocks, ladder_ints, cycle_ints):
    part = jax.ShapeDtypeStruct((NY, PACKED, TILE), F32)
    part_spec = pl.BlockSpec((NY, GROUP * SHARE, TILE), lambda g, i: (0, g, 0))
    return pl.pallas_call(
        ladder_kernel,
        out_shape=(part, part),
        grid_spec=pltpu.PrefetchScalarGridSpec(
            num_scalar_prefetch=1,
            grid=(COLS // GROUP,),
            in_specs=[pl.BlockSpec(memory_space=pl.ANY)] * 8
            + [
                pl.BlockSpec((GROUP, 1, LADDER, TILE, TILE), lambda g, i: (g, 0, 0, 0, 0)),
                pl.BlockSpec((GROUP, 1, CYCLE, TILE, TILE), lambda g, i: (g, 0, 0, 0, 0)),
            ],
            out_specs=(part_spec, part_spec),
            scratch_shapes=[
                pltpu.VMEM((65, ROWS, TILE), BF16),
                pltpu.VMEM((ROWS, TILE), F32),
                pltpu.SemaphoreType.DMA((8,)),
            ],
        ),
        compiler_params=pltpu.CompilerParams(vmem_limit_bytes=24 << 20),
        name="products",
    )(index, *blocks, ladder_ints, cycle_ints)


def add_kernel(a, b, *outs):
    for q, out in enumerate(outs):
        out[...] = a[q] + b[q]


def add_pair(a, b):
    return pl.pallas_call(
        add_kernel,
        out_shape=(jax.ShapeDtypeStruct((PACKED, TILE), F32),) * NY,
        name="add_pair",
    )(a, b)


def finish_kernel(a, b, c, d, bare, denominator, out):
    for col in range(COLS):
        rows = pl.ds(col * SHARE, SHARE)
        summed = (a[rows, :] + b[rows, :]) + (c[rows, :] + d[rows, :])
        residual = bare[col].astype(F32) + summed
        out[col] = (residual / denominator[col]).astype(BF16)


def finish(parts, bare, denominator):
    return pl.pallas_call(
        finish_kernel,
        out_shape=jax.ShapeDtypeStruct((COLS, SHARE, TILE), BF16),
        name="finish",
    )(*parts, bare, denominator)


def local(
    amplitudes,
    ladder_rows,
    ladder_ints,
    cycle_rows,
    cycle_ints,
    bare_ints,
    occ_energy,
    vir_energy,
    block_tiles,
):
    rep = lax.axis_index("rep")
    proc = lax.axis_index("proc")
    here_x, here_z = proc // NZ, proc % NZ

    mine = pick(amplitudes, rep.astype(jnp.int32).reshape(1))
    za1, zb1 = along_z(mine, -1), along_z(mine, 1)
    za2, zb2 = along_z(mine, -2), along_z(mine, 2)
    near = jnp.stack([mine, za1, zb1, za2, zb2]).reshape(10, ROWS, TILE)
    za3, zb3 = along_z(za2, -1), along_z(zb2, 1)
    z4 = along_z(za2, -2)
    xa_near, xb_near = along_x(near, -1), along_x(near, 1)
    far = jnp.stack([za3, zb3, z4]).reshape(6, ROWS, TILE)
    xa_far, xb_far = along_x(far, -1), along_x(far, 1)
    x2_near = along_x(xa_near, -1)
    x2_far = along_x(xb_far, 1)
    blocks = (near, far, xa_near, xa_far, x2_near, x2_far, xb_near, xb_far)

    tile = jnp.concatenate([ladder_rows[:, 0], cycle_rows[:, 0]], axis=1)
    dx = (tile // (16 * NZ) - here_x) % NX
    dz = ((tile // 16) % NZ - here_z) % NZ
    near_by = jnp.minimum(dz, NZ - dz)
    place = jnp.where(dz == 0, 0, 2 * near_by - 1 + (dz > NZ // 2))
    slot = (dx * NZ + place) * 2 + (tile // 8) % 2
    index = jnp.where(tile >= 0, slot, 64).astype(jnp.int32).reshape(-1)

    columns = proc * COLS + jnp.arange(COLS, dtype=jnp.int32)
    bounds = jnp.cumsum(block_tiles)
    irreps = jnp.sum((columns[:, None] >= bounds[None, :]).astype(jnp.int32), axis=1)
    selector = irreps[:, None] == jnp.arange(block_tiles.shape[0], dtype=jnp.int32)[None, :]
    occ_mine = lax.dynamic_slice_in_dim(occ_energy, rep * SHARE, SHARE, 1)
    occ_rows = jnp.sum(jnp.where(selector[:, :, None], occ_mine[None], 0.0), axis=1)
    denominator = vir_energy[:, None, :] - occ_rows[:, :, None]

    keep, send = ladder(index, blocks, ladder_ints, cycle_ints)
    own, up, across, down = add_pair(keep, other_core(send))
    parts = (own, along_y(up, 1), along_y(down, -1), along_y(across, 2))
    return finish(parts, bare_ints, denominator)


def solution(mesh):
    return jax.shard_map(
        local,
        mesh=mesh,
        in_specs=(
            P("proc", None, None),
            P("proc", "rep", None),
            P("proc", "rep", None, None, None),
            P("proc", "rep", None),
            P("proc", "rep", None, None, None),
            P("proc", "rep", None),
            P(),
            P("proc", None),
            P(),
        ),
        out_specs=P("proc", "rep", None),
        check_vma=False,
    )
```
